32 devices in a mesh: cand: 16 (over z, x, core), tp: 2 (over y).
Axes of the slice: x: 2, y: 2, z: 4, core: 2. Of those that a mesh axis runs over, the one named last changes fastest.
Arguments:
- hidden_in: bfloat16 [128, 2, 8192], P('cand'), may hold values from -4 to 4
- queries: bfloat16 [128, 2, 32, 128], P('cand', None, 'tp'), may hold values from -128 to 128
- new_kv: bfloat16 [128, 2, 8, 2, 128], P('cand', None, 'tp'), may hold values from -5 to 5
- kv_cache: bfloat16 [128, 8, 2, 512, 128], P('cand', 'tp'), may hold values from -6 to 6
- lengths: int32 [128], P('cand'), may hold values from 128 to 512, as said below
- winner: int32 [8], replicated, may hold values from 0 to 15
- out_values: bfloat16 [4096, 8192], P('tp'), may hold values from -4 to 4
- out_scales: float32 [32, 64], P('tp'), may hold values from 0.008 to 0.032
Outputs:
- mixed: bfloat16 [128, 2, 8192], P('cand')
The draws below stay inside these ranges and needn't reach their ends.
Inputs may be any that keep to these rules, and one draw needn't show every extreme that they name: `lengths`: every draw has some row with exactly 512 live slots.
All inputs are finite; a program needn't handle non-finite values.
Results may differ from the reference program's by a relative error of at most 0.013.
Values may be sent and summed in bfloat16 or wider, within the bound.
A program may use at most 128 MiB of HBM per device.

```python
import math
import jax
import jax.numpy as jnp
from jax import lax

D = 8192
H = 32
KVH = 8
HD = 128
PROB = 8
CACHE = 512
BLOCK = 64
STEPS = 2
SB = 128
ROWS = 128
N_CAND = 16


def draw_kv_cache(key, part):
    shape = (ROWS, KVH, 2, CACHE, HD)
    filled = jnp.clip(jax.random.normal(jax.random.fold_in(key, 502), shape, jnp.float32), -5.0, 5.0)
    return filled.astype(jnp.bfloat16)


def draw_queries(key, part):
    shape = (ROWS, STEPS, H, HD)
    entries = jnp.clip(2.0 * jax.random.normal(jax.random.fold_in(key, 503), shape, jnp.float32), -12.0, 12.0)
    return entries.astype(jnp.bfloat16)


def draw_lengths(key, part):
    devices_count = ROWS // PROB
    tier = jax.random.randint(jax.random.fold_in(key, 506), (devices_count,), 1, 5)
    ceiling = jnp.maximum(2 * BLOCK, CACHE * tier // 4)
    per_row = jnp.repeat(ceiling, PROB)
    drawn = jax.random.randint(jax.random.fold_in(key, 507), (ROWS,), 2 * BLOCK, per_row + 1)
    longest = jax.random.randint(jax.random.fold_in(key, 508), (), 0, ROWS)
    return jnp.where(jnp.arange(ROWS) == longest, CACHE, drawn).astype(jnp.int32)


def place_ends(array, own_key, low, largest):
    longest = array.shape.index(max(array.shape))
    spots = []
    for shift in (0, 1):
        where = [jax.random.randint(jax.random.fold_in(own_key, axis), (), 0, length) for axis, length in enumerate(array.shape)]
        where[longest] = (where[longest] + shift) % array.shape[longest]
        spots.append(tuple(where))
    return array.at[spots[0]].set(low).at[spots[1]].set(largest)


def block_scale(stream_key, extent, shards, least, high):
    def one(dim, parts):
        steps = jax.random.uniform(jax.random.fold_in(jax.random.fold_in(stream_key, 6), dim), (parts,), jnp.float32, least / len(shards), high / len(shards))
        return jnp.repeat(jnp.exp(steps), extent[dim] // parts).reshape((-1,) + (1,) * (len(extent) - dim - 1))

    level = one(*shards[0])
    for cut in shards[1:]:
        level = level * one(*cut)
    return level


def scatter_about(rng, extent, width, reach, pieces=(), held_as=jnp.bfloat16):
    level = block_scale(rng, extent, pieces, -0.22, 0.18) if pieces else 1.0
    values = jax.random.normal(rng, extent, jnp.float32) * width * level
    return jnp.minimum(jnp.maximum(values, -reach), reach).astype(held_as)


def setup_inputs(seed: int = 0) -> dict:
    arg_keys = jax.random.split(jax.random.key(seed), 9)
    return {
        "hidden_in": scatter_about(arg_keys[0], (ROWS, STEPS, D), 0.5, 4.0, ((0, 16),)),
        "queries": draw_queries(jax.random.fold_in(arg_keys[8], 71), 0),
        "new_kv": scatter_about(arg_keys[2], (ROWS, STEPS, KVH, 2, HD), 1.0, 5.0, ((0, 16), (2, 2))),
        "kv_cache": draw_kv_cache(jax.random.fold_in(arg_keys[8], 71), 0),
        "lengths": draw_lengths(jax.random.fold_in(arg_keys[8], 71), 0),
        "winner": place_ends(jax.random.randint(arg_keys[5], (PROB,), 0, N_CAND), jax.random.fold_in(arg_keys[5], 1), 0, N_CAND - 1).astype(jnp.int32),
        "out_values": scatter_about(arg_keys[6], (H * HD, D), 1.0, 4.0, ((0, 2),)),
        "out_scales": jnp.clip(jnp.exp(math.log(0.032) - 1.3862944 * jax.random.uniform(arg_keys[7], (H * HD // SB, D // SB), jnp.float32) ** block_scale(arg_keys[7], (H * HD // SB, D // SB), ((0, 2),), -0.2, 0.2)), 0.008, 0.032),
    }


def reference(hidden_in, queries, new_kv, kv_cache, lengths, winner, out_values, out_scales):
    group = H // KVH
    factor = 1.0 / math.sqrt(HD)
    positions = jnp.arange(CACHE, dtype=jnp.int32)
    causal = jnp.arange(STEPS, dtype=jnp.int32)[None, :] <= jnp.arange(STEPS, dtype=jnp.int32)[:, None]

    def one_row(row):
        problem = row % PROB
        source = winner[problem] * PROB + problem
        src_len = lengths[source]
        own_len = lengths[row]
        block = lax.dynamic_slice_in_dim(kv_cache[source], (src_len - BLOCK).astype(jnp.int32), BLOCK, 2)
        cache = lax.dynamic_update_slice_in_dim(kv_cache[row], block, (own_len - BLOCK).astype(jnp.int32), 2)
        query = queries[row].astype(jnp.float32).reshape(STEPS, KVH, group, HD)
        fresh = jnp.transpose(new_kv[row], (1, 2, 0, 3))
        keys = jnp.concatenate([cache[:, 0], fresh[:, 0]], axis=1).astype(jnp.float32)
        values = jnp.concatenate([cache[:, 1], fresh[:, 1]], axis=1).astype(jnp.float32)
        scores = jnp.einsum('tkgd,kjd->tkgj', query, keys) * factor
        old_valid = jnp.broadcast_to(positions[None, :] < own_len, (STEPS, CACHE))
        valid = jnp.concatenate([old_valid, causal], axis=1)
        scores = jnp.where(valid[:, None, None, :], scores, -jnp.inf)
        peak = lax.optimization_barrier(jnp.max(scores, axis=-1, keepdims=True))
        expo = jnp.exp(scores - peak)
        weights = (expo / lax.optimization_barrier(jnp.sum(expo, axis=-1, keepdims=True))).astype(jnp.bfloat16)
        attended = jnp.einsum('tkgj,kjd->tkgd', weights.astype(jnp.float32), values)
        return attended.astype(jnp.bfloat16).reshape(STEPS, H * HD)
    attended = lax.map(one_row, jnp.arange(ROWS, dtype=jnp.int32))
    flat = attended.reshape(ROWS * STEPS, H * HD)

    def add_block(index, term):
        piece = lax.dynamic_slice_in_dim(flat, index * SB, SB, 1)
        weight_rows = lax.dynamic_slice_in_dim(out_values, index * SB, SB, 0)
        scale = jnp.repeat(lax.dynamic_index_in_dim(out_scales, index, 0, keepdims=False), SB)
        return term + jnp.dot(piece, weight_rows, preferred_element_type=jnp.float32) * scale[None, :]
    term = lax.fori_loop(0, H * HD // SB, add_block, jnp.zeros((ROWS * STEPS, D), jnp.float32))
    result = (hidden_in.reshape(ROWS * STEPS, D).astype(jnp.float32) + term).astype(jnp.bfloat16)
    return result.reshape(ROWS, STEPS, D)
```

```python
import functools
import math

import jax
import jax.numpy as jnp
from jax import lax
from jax.experimental import pallas as pl
from jax.experimental.pallas import tpu as pltpu
from jax.sharding import PartitionSpec as P

BLOCK = 64
LAG_IN = 4
LAG_OUT = 9
PAIR = 2
LOW = -1e30
MESH = pl.DeviceIdType.MESH


def kernel(
    cand_n, tp_n, tile, split,
    lengths, winner, scales, queries_hbm, fresh_hbm, hidden_hbm, cache_hbm, weights_hbm, out_hbm,
    caches, weights, queries, fresh, hidden, out, blocks, got, own,
    near0, up0, far0, down0, mid, near1, up1, far1, down1,
    fork, top_s, sum_s, acc_s, att, lhs, parts, other,
    cache_sem, weight_sem, small_sem, out_sem, send_sem, recv_sem,
    part_send, part_recv, swap_send, swap_recv, other_send,
):
    me = lax.axis_index("cand")
    tp_me = lax.axis_index("tp")
    problems = len(caches)
    kv_here, _, slots, head_dim = caches[0].shape
    steps_heads = queries.shape[1]
    heads = weights.shape[0] // head_dim
    steps = steps_heads // heads
    group = heads // kv_here
    groups = problems // PAIR
    rows = PAIR * steps
    chunks = groups * split
    core = lax.rem(me, 2)
    chip = lax.div(me, 2)
    outer_len = 4
    inner_len = cand_n // 2 // outer_len
    inner_at = lax.rem(chip, inner_len)
    outer_at = lax.div(chip, inner_len)
    sibling = me + 1 - 2 * core

    def ends(at, length, stride):
        low_side = at < length // 2
        step = jnp.where(low_side, stride, -stride)
        has_near = jnp.logical_and(at > 0, at < length - 1)
        crosses = jnp.logical_or(at == length // 2 - 1, at == length // 2)
        return length, has_near, crosses, me + step, me - step

    inner = ends(inner_at, inner_len, 2)
    outer = ends(outer_at, outer_len, 2 * inner_len)

    pieces = weight_sem.shape[0]
    piece = weights.shape[0] // pieces

    def cache_copy(p):
        return pltpu.make_async_copy(cache_hbm.at[p], caches[p], cache_sem.at[p])

    def weight_copy(i):
        at = pl.ds(i * piece, piece)
        columns = pl.ds(pl.multiple_of(core * weights.shape[1], tile), weights.shape[1])
        return pltpu.make_async_copy(weights_hbm.at[at, columns], weights.at[at], weight_sem.at[i])

    queries_copy = pltpu.make_async_copy(queries_hbm, queries, small_sem.at[0])
    fresh_copy = pltpu.make_async_copy(fresh_hbm, fresh, small_sem.at[1])
    hidden_copy = pltpu.make_async_copy(hidden_hbm, hidden, small_sem.at[2])

    for p in range(PAIR):
        cache_copy(p).start()
    queries_copy.start()
    fresh_copy.start()
    for p in range(PAIR, problems):
        cache_copy(p).start()

    barrier = pltpu.get_barrier_semaphore()

    def greet(**where):
        pl.semaphore_signal(barrier, inc=1, device_id=where, device_id_type=MESH)

    greet(cand=sibling)
    count = 1 + 2 * (tp_n - 1)
    for _, has_near, _, far, near in (inner, outer):
        greet(cand=far)

        @pl.when(has_near)
        def _(near=near):
            greet(cand=near)

        count = count + 1 + has_near.astype(jnp.int32)
    for k in range(1, tp_n):
        greet(tp=lax.rem(tp_me + k, tp_n))
        greet(cand=sibling, tp=lax.rem(tp_me + k, tp_n))

    def remote(src, dst, kind, j, target):
        return pltpu.make_async_remote_copy(
            src_ref=src, dst_ref=dst, send_sem=send_sem.at[kind, j],
            recv_sem=recv_sem.at[kind, j], device_id={"cand": target}, device_id_type=MESH,
        )

    def place(side, j):
        return (PAIR * lax.div(j, split) + side) * split + lax.rem(j, split)

    def sibling_copy(j):
        return remote(blocks.at[place(1 - core, j)], got.at[j], 0, j, sibling)

    def loop(body, first, last):
        def step(j, carry):
            body(j)
            return carry

        lax.fori_loop(first, last, step, 0)

    def make_line(line, kind, base_ref, near_ref, up_ref, far_ref, down_ref):
        length, has_near, crosses, far_id, near_id = line
        short = length == 2
        if short:
            up_ref = base_ref

        def to_far_in(j):
            return remote(up_ref.at[j], near_ref.at[j], kind, j, far_id)

        def to_far_cross(j):
            return remote(up_ref.at[j], far_ref.at[j], kind + 1, j, far_id)

        def to_near(j):
            return pltpu.make_async_remote_copy(
                src_ref=down_ref.at[j], dst_ref=far_ref.at[j], send_sem=send_sem.at[kind + 2, j],
                recv_sem=recv_sem.at[kind + 1, j], device_id={"cand": near_id}, device_id_type=MESH,
            )

        def climb(j):
            if short:
                to_far_cross(j).start()
                return

            @pl.when(has_near)
            def _():
                to_far_in(j).wait_recv()
                up_ref[j] = base_ref[j] + near_ref[j]

            @pl.when(jnp.logical_not(has_near))
            def _():
                up_ref[j] = base_ref[j]

            @pl.when(crosses)
            def _():
                to_far_cross(j).start()

            @pl.when(jnp.logical_not(crosses))
            def _():
                to_far_in(j).start()

        def settle(j):
            to_far_cross(j).wait_recv()
            if not short:
                @pl.when(has_near)
                def _():
                    down_ref[j] = base_ref[j] + far_ref[j]
                    to_near(j).start()

            return up_ref[j] + far_ref[j]

        def drain(j):
            if short:
                to_far_cross(j).wait_send()
                return

            @pl.when(crosses)
            def _():
                to_far_cross(j).wait_send()

            @pl.when(jnp.logical_not(crosses))
            def _():
                to_far_in(j).wait_send()

            @pl.when(has_near)
            def _():
                to_near(j).wait_send()

        return climb, settle, drain

    climb0, settle0, drain0 = make_line(inner, 1, own, near0, up0, far0, down0)
    climb1, settle1, drain1 = make_line(outer, 4, mid, near1, up1, far1, down1)

    def enter(j):
        sibling_copy(j).wait_recv()
        own[j] = blocks[place(core, j)] + got[j]
        climb0(j)

    factor = 1.0 / math.sqrt(head_dim)

    def row_of(width):
        return lax.broadcasted_iota(jnp.int32, (steps_heads, width), 0)

    def col_of(width):
        return lax.broadcasted_iota(jnp.int32, (steps_heads, width), 1)

    def score(q, keys):
        return lax.dot_general(q, keys, (((1,), (1,)), ((), ())), preferred_element_type=jnp.float32) * factor

    pick_row = lax.broadcasted_iota(jnp.int32, (BLOCK, slots), 0)
    pick_col = lax.broadcasted_iota(jnp.int32, (BLOCK, slots), 1)
    hs = kv_here // split

    def pick(p):
        hit = jnp.logical_and(
            pick_col - pick_row == lengths[p] - BLOCK, jnp.zeros_like(pick_col) + winner[p] == me
        )
        chosen = hit.astype(jnp.float32).astype(jnp.bfloat16)
        for h in range(kv_here):
            for kv in range(2):
                blocks[p * split + h // hs, h % hs, kv] = jnp.dot(
                    chosen, caches[p][h, kv], preferred_element_type=jnp.float32
                ).astype(jnp.bfloat16)

    def local_part(p):
        q = queries[p]
        s = score(q, caches[p][:, 0].reshape(kv_here * slots, head_dim))
        row, col = row_of(kv_here * slots), col_of(kv_here * slots)
        mine = lax.div(lax.rem(row, heads), group) == lax.div(col, slots)
        s = jnp.where(jnp.logical_and(mine, lax.rem(col, slots) < lengths[p] - BLOCK), s, LOW)
        both = fresh[p]
        n = score(q, both)
        width = both.shape[0]
        row, col = row_of(width), col_of(width)
        mine = lax.div(lax.rem(row, heads), group) == lax.rem(lax.div(col, 2), kv_here)
        mine = jnp.logical_and(mine, lax.rem(col, 2) == 0)
        n = jnp.where(jnp.logical_and(mine, lax.div(col, 2 * kv_here) <= lax.div(row, heads)), n, LOW)
        wide = both.astype(jnp.float32)
        values = jnp.concatenate([wide[1:], wide[:1]], 0).astype(jnp.bfloat16)
        top = jnp.maximum(jnp.max(s, 1, keepdims=True), jnp.max(n, 1, keepdims=True))
        s = jnp.exp(s - top)
        n = jnp.exp(n - top)
        top_s[p] = jnp.broadcast_to(top, (steps_heads, head_dim))
        sum_s[p] = jnp.broadcast_to(jnp.sum(s, 1, keepdims=True) + jnp.sum(n, 1, keepdims=True), (steps_heads, head_dim))
        acc_s[p] = jnp.dot(
            s.astype(jnp.bfloat16), caches[p][:, 1].reshape(kv_here * slots, head_dim),
            preferred_element_type=jnp.float32,
        ) + jnp.dot(n.astype(jnp.bfloat16), values, preferred_element_type=jnp.float32)

    for g in range(groups):
        for p in range(PAIR * g, PAIR * (g + 1)):
            cache_copy(p).wait()
            pick(p)
        if g == 0:
            pl.semaphore_wait(barrier, count)
        loop(lambda j: sibling_copy(j).start(), g * split, (g + 1) * split)
        if g > 0:
            loop(enter, (g - 1) * split, g * split)
        else:
            queries_copy.wait()
            fresh_copy.wait()
        if g == groups - 1:
            for i in range(pieces):
                weight_copy(i).start()
            hidden_copy.start()
        for p in range(PAIR * g, PAIR * (g + 1)):
            local_part(p)
    loop(enter, (groups - 1) * split, chunks)

    def turn(j):
        mid[j] = settle0(j)
        climb1(j)

    def fork_copy(j):
        at = place(core, j)
        return remote(fork.at[at], fork.at[at], 7, j, sibling)

    def finish(j):
        fork[place(core, j)] = settle1(j)
        fork_copy(j).start()

    def closing(j):
        remote(got.at[j], fork.at[place(1 - core, j)], 7, j, sibling).wait_recv()

    def fork_part(p, slot):
        q = queries[p]
        both = fork[pl.ds(p * split, split)]
        keys = both[:, :, 0].reshape(kv_here * BLOCK, head_dim)
        values = both[:, :, 1].reshape(kv_here * BLOCK, head_dim)
        s = score(q, keys)
        row, col = row_of(kv_here * BLOCK), col_of(kv_here * BLOCK)
        mine = lax.div(lax.rem(row, heads), group) == lax.div(col, BLOCK)
        s = jnp.where(mine, s, LOW)
        before = top_s[p]
        top = jnp.maximum(before, jnp.max(s, 1, keepdims=True))
        s = jnp.exp(s - top[:, :1])
        scale = jnp.exp(before - top)
        total = sum_s[p] * scale + jnp.sum(s, 1, keepdims=True)
        acc = acc_s[p] * scale + jnp.dot(s.astype(jnp.bfloat16), values, preferred_element_type=jnp.float32)
        att[pl.ds(slot * steps_heads, steps_heads), :] = acc / total

    pairs = heads // 2

    def swap_copy(g):
        return pltpu.make_async_remote_copy(
            src_ref=lhs.at[0, g], dst_ref=lhs.at[1, g], send_sem=swap_send.at[g], recv_sem=swap_recv.at[g],
            device_id={"cand": sibling}, device_id_type=MESH,
        )

    def fork_group(g):
        loop(closing, g * split, (g + 1) * split)
        for i in range(PAIR):
            fork_part(PAIR * g + i, i)
        empty = jnp.zeros((rows, head_dim), jnp.float32)
        for i in range(pairs):
            a = att[pl.ds(2 * i, rows, stride=heads), :]
            b = att[pl.ds(2 * i + 1, rows, stride=heads), :]
            lhs[0, g, i] = jnp.concatenate(
                [jnp.concatenate([a, empty], 1), jnp.concatenate([empty, b], 1)], 0
            ).astype(jnp.bfloat16)
        swap_copy(g).start()

    tiles = parts.shape[2]
    here_tiles = tiles // 2
    per = tile // head_dim

    def part_copy(g, t, k):
        at = core * here_tiles + t
        return pltpu.make_async_remote_copy(
            src_ref=parts.at[tp_me, g, at], dst_ref=parts.at[tp_me, g, at], send_sem=part_send.at[k - 1, g, t],
            recv_sem=part_recv.at[tp_me, g, at], device_id={"tp": lax.rem(tp_me + k, tp_n)},
            device_id_type=MESH,
        )

    def other_copy(g, t, k):
        at = core * here_tiles + t
        return pltpu.make_async_remote_copy(
            src_ref=other.at[g, t], dst_ref=parts.at[tp_me, g, at], send_sem=other_send.at[k, g, t],
            recv_sem=part_recv.at[tp_me, g, at],
            device_id={"cand": sibling, "tp": lax.rem(tp_me + k, tp_n)}, device_id_type=MESH,
        )

    def project(g, t):
        at = pl.ds(pl.multiple_of(t * tile, tile), tile)
        first_scale = (core * here_tiles + t) * per
        row = lax.broadcasted_iota(jnp.int32, (4 * rows, head_dim), 0)
        even = lax.rem(row, 2 * rows) < rows
        total = [jnp.zeros((4 * rows, head_dim), jnp.float32) for _ in range(per)]
        for i in range(pairs):
            product = jnp.dot(
                lhs[:, g, i].reshape(4 * rows, 2 * head_dim),
                weights[pl.ds(2 * i * head_dim, 2 * head_dim), at], preferred_element_type=jnp.float32,
            )
            for c in range(per):
                scale = jnp.where(even, scales[2 * i, first_scale + c], scales[2 * i + 1, first_scale + c])
                total[c] = total[c] + product[:, c * head_dim:(c + 1) * head_dim] * scale
        whole = jnp.concatenate(total, 1).reshape(2, 2, rows, tile)
        whole = (whole[:, 0] + whole[:, 1]).astype(jnp.bfloat16)
        parts[tp_me, g, core * here_tiles + t] = whole[0]
        other[g, t] = whole[1]
        for k in range(1, tp_n):
            other_copy(g, t, k).start()
            part_copy(g, t, k).start()
        other_copy(g, t, 0).start()

    share = here_tiles // split

    def project_piece(g, at):
        @pl.when(at == 0)
        def _():
            @pl.when(g == 0)
            def _():
                for i in range(pieces):
                    weight_copy(i).wait()

            swap_copy(g).wait_recv()

        loop(lambda t: project(g, t), at * share, (at + 1) * share)

    def out_copy(g):
        at = pl.ds(PAIR * g, PAIR)
        return pltpu.make_async_copy(out.at[at], out_hbm.at[at], out_sem.at[g])

    def gather_tile(g, t):
        at = pl.ds(pl.multiple_of(t * tile, tile), tile)

        def arrived(source):
            pltpu.make_async_remote_copy(
                src_ref=other.at[0, 0], dst_ref=parts.at[source, g, t], send_sem=swap_send.at[0],
                recv_sem=part_recv.at[source, g, t], device_id={"cand": sibling}, device_id_type=MESH,
            ).wait_recv()

        @pl.when(lax.div(t, here_tiles) != core)
        def _():
            arrived(tp_me)

        for k in range(1, tp_n):
            arrived(lax.rem(tp_me + k, tp_n))
        total = parts[0, g, t].astype(jnp.float32)
        for k in range(1, tp_n):
            total = total + parts[k, g, t].astype(jnp.float32)
        for i in range(PAIR):
            mixed = hidden[PAIR * g + i, :, at].astype(jnp.float32) + total[i * steps:(i + 1) * steps]
            out[PAIR * g + i, :, at] = mixed.astype(jnp.bfloat16)

    def gather(g):
        @pl.when(g == 0)
        def _():
            hidden_copy.wait()

        def both_halves(t):
            gather_tile(g, t)
            gather_tile(g, t + here_tiles)

        loop(both_halves, 0, here_tiles)
        out_copy(g).start()

    fork_at = split + 1
    project_at = fork_at + 2
    gather_at = project_at + split + 3

    def within(at, length):
        return jnp.logical_and(at >= 0, at < length)

    def advance(i):
        @pl.when(i < chunks)
        def _():
            turn(i)

        @pl.when(jnp.logical_and(outer[1], within(i - LAG_IN, chunks)))
        def _():
            finish(i - LAG_IN)

        now = i - LAG_OUT

        @pl.when(jnp.logical_and(jnp.logical_not(outer[1]), within(now, chunks)))
        def _():
            finish(now)

        def starts(at):
            return jnp.logical_and(within(now - at, chunks), lax.rem(now - at + chunks, split) == 0)

        @pl.when(starts(fork_at))
        def _():
            fork_group(lax.div(now - fork_at, split))

        @pl.when(within(now - project_at, chunks))
        def _():
            at = now - project_at
            project_piece(lax.div(at, split), lax.rem(at, split))

        @pl.when(starts(gather_at))
        def _():
            gather(lax.div(now - gather_at, split))

    loop(advance, 0, LAG_OUT + gather_at + chunks)

    def rest(j):
        sibling_copy(j).wait_send()
        drain0(j)
        drain1(j)
        fork_copy(j).wait_send()

    loop(rest, 0, chunks)

    def rest_group(g):
        swap_copy(g).wait_send()

        def rest_parts(t):
            other_copy(g, t, 0).wait_send()
            for k in range(1, tp_n):
                part_copy(g, t, k).wait_send()
                other_copy(g, t, k).wait_send()

        loop(rest_parts, 0, here_tiles)
        out_copy(g).wait()

    loop(rest_group, 0, groups)


def local(cand_n, tp_n, hidden_in, queries, new_kv, kv_cache, lengths, winner, out_values, out_scales):
    problems, kv_here, _, slots, head_dim = kv_cache.shape
    steps, heads = queries.shape[1:3]
    depth, width = out_values.shape
    groups = problems // PAIR
    rows = PAIR * steps
    split = 4 if kv_here % 4 == 0 else 1
    hs = kv_here // split
    chunks = groups * split
    tile = 512
    tiles = width // tile
    flat = queries.reshape(problems, steps * heads, head_dim)
    fresh = new_kv.reshape(problems, steps * kv_here * 2, head_dim)
    smem = pl.BlockSpec(memory_space=pltpu.SMEM)
    hbm = pl.BlockSpec(memory_space=pl.ANY)
    line = pltpu.VMEM((chunks, hs, 2, BLOCK, head_dim), jnp.bfloat16)
    none = pltpu.VMEM((1, hs, 2, BLOCK, head_dim), jnp.bfloat16)
    short = cand_n // 2 // 4 == 2
    spare = none if short else line
    every = pltpu.VMEM((problems * split, hs, 2, BLOCK, head_dim), jnp.bfloat16)
    stat = pltpu.VMEM((problems, steps * heads, head_dim), jnp.float32)
    dma = pltpu.SemaphoreType.DMA
    return pl.pallas_call(
        functools.partial(kernel, cand_n, tp_n, tile, split),
        out_shape=jax.ShapeDtypeStruct(hidden_in.shape, jnp.bfloat16),
        in_specs=[smem, smem, smem, hbm, hbm, hbm, hbm, hbm],
        out_specs=hbm,
        scratch_shapes=[
            [pltpu.VMEM(kv_cache.shape[1:], jnp.bfloat16)] * problems,
            pltpu.VMEM((depth, width // 2), jnp.bfloat16),
            pltpu.VMEM(flat.shape, jnp.bfloat16),
            pltpu.VMEM(fresh.shape, jnp.bfloat16),
            pltpu.VMEM(hidden_in.shape, jnp.bfloat16),
            pltpu.VMEM(hidden_in.shape, jnp.bfloat16),
            every, line, line,
            spare, spare, line, spare,
            *[line] * 5,
            every, stat, stat, stat,
            pltpu.VMEM((PAIR * steps * heads, head_dim), jnp.float32),
            pltpu.VMEM((2, groups, heads // 2, 2 * rows, 2 * head_dim), jnp.bfloat16),
            pltpu.VMEM((tp_n, groups, tiles, rows, tile), jnp.bfloat16),
            pltpu.VMEM((groups, tiles // 2, rows, tile), jnp.bfloat16),
            dma((problems,)), dma((8,)), dma((3,)), dma((groups,)), dma((8, chunks)), dma((8, chunks)),
            dma((max(tp_n - 1, 1), groups, tiles // 2)), dma((tp_n, groups, tiles)),
            dma((groups,)), dma((groups,)), dma((tp_n, groups, tiles // 2)),
        ],
        compiler_params=pltpu.CompilerParams(
            collective_id=0, has_side_effects=True, vmem_limit_bytes=67043328 - (2 << 20)
        ),
    )(lengths, winner, out_scales, flat, fresh, hidden_in, kv_cache, out_values)


def solution(mesh):
    placed = (
        P("cand", None, None),
        P("cand", None, "tp", None),
        P("cand", None, "tp", None, None),
        P("cand", "tp", None, None, None),
        P("cand"),
        P(),
        P("tp", None),
        P("tp", None),
    )
    return jax.shard_map(
        functools.partial(local, mesh.shape["cand"], mesh.shape["tp"]),
        mesh=mesh, in_specs=placed, out_specs=P("cand", None, None), check_vma=False,
    )
```

```python
import functools
import math

import jax
import jax.numpy as jnp
from jax import lax
from jax.experimental import pallas as pl
from jax.experimental.pallas import tpu as pltpu
from jax.sharding import PartitionSpec as P

BLOCK = 64
LAG_IN = 4
LAG_OUT = 12
PAIR = 2
GROUP = 4
LOW = -1e30
MESH = pl.DeviceIdType.MESH


def kernel(
    cand_n, tp_n, tile, split,
    lengths, winner, scales, queries_hbm, fresh_hbm, hidden_hbm, cache_hbm, weights_hbm, out_hbm,
    caches, weights, queries, fresh, hidden, out, blocks, got, own,
    near0, up0, far0, down0, mid, near1, up1, far1, down1,
    fork, top_s, sum_s, acc_s, att, lhs, parts, other,
    cache_sem, weight_sem, small_sem, out_sem, send_sem, recv_sem,
    part_send, part_recv, swap_send, swap_recv, other_send,
):
    me = lax.axis_index("cand")
    tp_me = lax.axis_index("tp")
    problems = len(caches)
    kv_here, _, slots, head_dim = caches[0].shape
    steps_heads = queries.shape[1]
    heads = weights.shape[0] // head_dim
    steps = steps_heads // heads
    group = heads // kv_here
    groups = problems // GROUP
    rows = GROUP * steps
    chunks = problems // PAIR * split
    span = GROUP // PAIR * split
    core = lax.rem(me, 2)
    chip = lax.div(me, 2)
    outer_len = 4
    inner_len = cand_n // 2 // outer_len
    inner_at = lax.rem(chip, inner_len)
    outer_at = lax.div(chip, inner_len)
    sibling = me + 1 - 2 * core

    def ends(at, length, stride):
        low_side = at < length // 2
        step = jnp.where(low_side, stride, -stride)
        has_near = jnp.logical_and(at > 0, at < length - 1)
        crosses = jnp.logical_or(at == length // 2 - 1, at == length // 2)
        return length, has_near, crosses, me + step, me - step

    inner = ends(inner_at, inner_len, 2)
    outer = ends(outer_at, outer_len, 2 * inner_len)

    pieces = weight_sem.shape[0]
    piece = weights.shape[0] // pieces

    def cache_copy(p):
        return pltpu.make_async_copy(cache_hbm.at[p], caches[p], cache_sem.at[p])

    def weight_copy(i):
        at = pl.ds(i * piece, piece)
        columns = pl.ds(pl.multiple_of(core * weights.shape[1], tile), weights.shape[1])
        return pltpu.make_async_copy(weights_hbm.at[at, columns], weights.at[at], weight_sem.at[i])

    queries_copy = pltpu.make_async_copy(queries_hbm, queries, small_sem.at[0])
    fresh_copy = pltpu.make_async_copy(fresh_hbm, fresh, small_sem.at[1])
    hidden_copy = pltpu.make_async_copy(hidden_hbm, hidden, small_sem.at[2])

    for p in range(PAIR):
        cache_copy(p).start()
    queries_copy.start()
    fresh_copy.start()
    for p in range(PAIR, problems):
        cache_copy(p).start()

    barrier = pltpu.get_barrier_semaphore()

    def greet(**where):
        pl.semaphore_signal(barrier, inc=1, device_id=where, device_id_type=MESH)

    greet(cand=sibling)
    count = 1 + 2 * (tp_n - 1)
    for _, has_near, _, far, near in (inner, outer):
        greet(cand=far)

        @pl.when(has_near)
        def _(near=near):
            greet(cand=near)

        count = count + 1 + has_near.astype(jnp.int32)
    for k in range(1, tp_n):
        greet(tp=lax.rem(tp_me + k, tp_n))
        greet(cand=sibling, tp=lax.rem(tp_me + k, tp_n))

    def remote(src, dst, kind, j, target):
        return pltpu.make_async_remote_copy(
            src_ref=src, dst_ref=dst, send_sem=send_sem.at[kind, j],
            recv_sem=recv_sem.at[kind, j], device_id={"cand": target}, device_id_type=MESH,
        )

    def place(side, j):
        return (PAIR * lax.div(j, split) + side) * split + lax.rem(j, split)

    def sibling_copy(j):
        return remote(blocks.at[place(1 - core, j)], got.at[j], 0, j, sibling)

    def loop(body, first, last):
        def step(j, carry):
            body(j)
            return carry

        lax.fori_loop(first, last, step, 0)

    def make_line(line, kind, base_ref, near_ref, up_ref, far_ref, down_ref):
        length, has_near, crosses, far_id, near_id = line
        short = length == 2
        if short:
            up_ref = base_ref

        def to_far_in(j):
            return remote(up_ref.at[j], near_ref.at[j], kind, j, far_id)

        def to_far_cross(j):
            return remote(up_ref.at[j], far_ref.at[j], kind + 1, j, far_id)

        def to_near(j):
            return pltpu.make_async_remote_copy(
                src_ref=down_ref.at[j], dst_ref=far_ref.at[j], send_sem=send_sem.at[kind + 2, j],
                recv_sem=recv_sem.at[kind + 1, j], device_id={"cand": near_id}, device_id_type=MESH,
            )

        def climb(j):
            if short:
                to_far_cross(j).start()
                return

            @pl.when(has_near)
            def _():
                to_far_in(j).wait_recv()
                up_ref[j] = base_ref[j] + near_ref[j]

            @pl.when(jnp.logical_not(has_near))
            def _():
                up_ref[j] = base_ref[j]

            @pl.when(crosses)
            def _():
                to_far_cross(j).start()

            @pl.when(jnp.logical_not(crosses))
            def _():
                to_far_in(j).start()

        def settle(j):
            to_far_cross(j).wait_recv()
            if not short:
                @pl.when(has_near)
                def _():
                    down_ref[j] = base_ref[j] + far_ref[j]
                    to_near(j).start()

            return up_ref[j] + far_ref[j]

        def drain(j):
            if short:
                to_far_cross(j).wait_send()
                return

            @pl.when(crosses)
            def _():
                to_far_cross(j).wait_send()

            @pl.when(jnp.logical_not(crosses))
            def _():
                to_far_in(j).wait_send()

            @pl.when(has_near)
            def _():
                to_near(j).wait_send()

        return climb, settle, drain

    climb0, settle0, drain0 = make_line(inner, 1, own, near0, up0, far0, down0)
    climb1, settle1, drain1 = make_line(outer, 4, mid, near1, up1, far1, down1)

    def enter(j):
        sibling_copy(j).wait_recv()
        own[j] = blocks[place(core, j)] + got[j]
        climb0(j)

    factor = 1.0 / math.sqrt(head_dim)

    def row_of(width):
        return lax.broadcasted_iota(jnp.int32, (steps_heads, width), 0)

    def col_of(width):
        return lax.broadcasted_iota(jnp.int32, (steps_heads, width), 1)

    def score(q, keys):
        return lax.dot_general(q, keys, (((1,), (1,)), ((), ())), preferred_element_type=jnp.float32) * factor

    pick_row = lax.broadcasted_iota(jnp.int32, (BLOCK, slots), 0)
    pick_col = lax.broadcasted_iota(jnp.int32, (BLOCK, slots), 1)
    hs = kv_here // split

    def pick(p):
        hit = jnp.logical_and(
            pick_col - pick_row == lengths[p] - BLOCK, jnp.zeros_like(pick_col) + winner[p] == me
        )
        chosen = hit.astype(jnp.float32).astype(jnp.bfloat16)
        for h in range(kv_here):
            for kv in range(2):
                blocks[p * split + h // hs, h % hs, kv] = jnp.dot(
                    chosen, caches[p][h, kv], preferred_element_type=jnp.float32
                ).astype(jnp.bfloat16)

    def local_part(p):
        q = queries[p]
        s = score(q, caches[p][:, 0].reshape(kv_here * slots, head_dim))
        row, col = row_of(kv_here * slots), col_of(kv_here * slots)
        mine = lax.div(lax.rem(row, heads), group) == lax.div(col, slots)
        s = jnp.where(jnp.logical_and(mine, lax.rem(col, slots) < lengths[p] - BLOCK), s, LOW)
        both = fresh[p]
        n = score(q, both)
        width = both.shape[0]
        row, col = row_of(width), col_of(width)
        mine = lax.div(lax.rem(row, heads), group) == lax.rem(lax.div(col, 2), kv_here)
        mine = jnp.logical_and(mine, lax.rem(col, 2) == 0)
        n = jnp.where(jnp.logical_and(mine, lax.div(col, 2 * kv_here) <= lax.div(row, heads)), n, LOW)
        wide = both.astype(jnp.float32)
        values = jnp.concatenate([wide[1:], wide[:1]], 0).astype(jnp.bfloat16)
        top = jnp.maximum(jnp.max(s, 1, keepdims=True), jnp.max(n, 1, keepdims=True))
        s = jnp.exp(s - top)
        n = jnp.exp(n - top)
        top_s[p] = jnp.broadcast_to(top, (steps_heads, head_dim))
        sum_s[p] = jnp.broadcast_to(jnp.sum(s, 1, keepdims=True) + jnp.sum(n, 1, keepdims=True), (steps_heads, head_dim))
        acc_s[p] = jnp.dot(
            s.astype(jnp.bfloat16), caches[p][:, 1].reshape(kv_here * slots, head_dim),
            preferred_element_type=jnp.float32,
        ) + jnp.dot(n.astype(jnp.bfloat16), values, preferred_element_type=jnp.float32)

    for g in range(problems // PAIR):
        for p in range(PAIR * g, PAIR * (g + 1)):
            cache_copy(p).wait()
            pick(p)
        if g == 0:
            pl.semaphore_wait(barrier, count)
        loop(lambda j: sibling_copy(j).start(), g * split, (g + 1) * split)
        if g > 0:
            loop(enter, (g - 1) * split, g * split)
    for i in range(pieces):
        weight_copy(i).start()
    hidden_copy.start()
    queries_copy.wait()
    fresh_copy.wait()
    early = problems // 2
    local_part(0)
    loop(enter, chunks - split, chunks)
    for p in range(1, early):
        local_part(p)

    def turn(j):
        mid[j] = settle0(j)
        climb1(j)

    def fork_copy(j):
        at = place(core, j)
        return remote(fork.at[at], fork.at[at], 7, j, sibling)

    def finish(j):
        fork[place(core, j)] = settle1(j)
        fork_copy(j).start()

    def closing(j):
        remote(got.at[j], fork.at[place(1 - core, j)], 7, j, sibling).wait_recv()

    def fork_part(p, slot):
        q = queries[p]
        both = fork[pl.ds(p * split, split)]
        keys = both[:, :, 0].reshape(kv_here * BLOCK, head_dim)
        values = both[:, :, 1].reshape(kv_here * BLOCK, head_dim)
        s = score(q, keys)
        row, col = row_of(kv_here * BLOCK), col_of(kv_here * BLOCK)
        mine = lax.div(lax.rem(row, heads), group) == lax.div(col, BLOCK)
        s = jnp.where(mine, s, LOW)
        before = top_s[p]
        top = jnp.maximum(before, jnp.max(s, 1, keepdims=True))
        s = jnp.exp(s - top[:, :1])
        scale = jnp.exp(before - top)
        total = sum_s[p] * scale + jnp.sum(s, 1, keepdims=True)
        acc = acc_s[p] * scale + jnp.dot(s.astype(jnp.bfloat16), values, preferred_element_type=jnp.float32)
        att[pl.ds(slot * steps_heads, steps_heads), :] = acc / total

    pairs = heads // 2

    def swap_copy(g):
        return pltpu.make_async_remote_copy(
            src_ref=lhs.at[0, g], dst_ref=lhs.at[1, g], send_sem=swap_send.at[g], recv_sem=swap_recv.at[g],
            device_id={"cand": sibling}, device_id_type=MESH,
        )

    def fork_group(g):
        loop(closing, g * span, (g + 1) * span)
        loop(lambda i: fork_part(GROUP * g + i, i), 0, GROUP)
        empty = jnp.zeros((rows, head_dim), jnp.float32)
        for i in range(pairs):
            a = att[pl.ds(2 * i, rows, stride=heads), :]
            b = att[pl.ds(2 * i + 1, rows, stride=heads), :]
            lhs[0, g, i] = jnp.concatenate(
                [jnp.concatenate([a, empty], 1), jnp.concatenate([empty, b], 1)], 0
            ).astype(jnp.bfloat16)
        swap_copy(g).start()

    tiles = parts.shape[2]
    here_tiles = tiles // 2
    per = tile // head_dim

    def part_copy(g, t, k):
        at = core * here_tiles + t
        return pltpu.make_async_remote_copy(
            src_ref=parts.at[tp_me, g, at], dst_ref=parts.at[tp_me, g, at], send_sem=part_send.at[k - 1, g, t],
            recv_sem=part_recv.at[tp_me, g, at], device_id={"tp": lax.rem(tp_me + k, tp_n)},
            device_id_type=MESH,
        )

    def other_copy(g, t, k):
        at = core * here_tiles + t
        return pltpu.make_async_remote_copy(
            src_ref=other.at[g, t], dst_ref=parts.at[tp_me, g, at], send_sem=other_send.at[k, g, t],
            recv_sem=part_recv.at[tp_me, g, at],
            device_id={"cand": sibling, "tp": lax.rem(tp_me + k, tp_n)}, device_id_type=MESH,
        )

    def project(g, t):
        at = pl.ds(pl.multiple_of(t * tile, tile), tile)
        first_scale = (core * here_tiles + t) * per
        row = lax.broadcasted_iota(jnp.int32, (4 * rows, head_dim), 0)
        even = lax.rem(row, 2 * rows) < rows
        total = [jnp.zeros((4 * rows, head_dim), jnp.float32) for _ in range(per)]
        for i in range(pairs):
            product = jnp.dot(
                lhs[:, g, i].reshape(4 * rows, 2 * head_dim),
                weights[pl.ds(2 * i * head_dim, 2 * head_dim), at], preferred_element_type=jnp.float32,
            )
            for c in range(per):
                scale = jnp.where(even, scales[2 * i, first_scale + c], scales[2 * i + 1, first_scale + c])
                total[c] = total[c] + product[:, c * head_dim:(c + 1) * head_dim] * scale
        whole = jnp.concatenate(total, 1).reshape(2, 2, rows, tile)
        whole = (whole[:, 0] + whole[:, 1]).astype(jnp.bfloat16)
        parts[tp_me, g, core * here_tiles + t] = whole[0]
        other[g, t] = whole[1]
        for k in range(1, tp_n):
            other_copy(g, t, k).start()
            part_copy(g, t, k).start()
        other_copy(g, t, 0).start()

    share = max(here_tiles // span, 1)
    turns = here_tiles // share

    def project_piece(g, at):
        @pl.when(at == 0)
        def _():
            if g == 0:
                for i in range(pieces):
                    weight_copy(i).wait()
            swap_copy(g).wait_recv()

        loop(lambda t: project(g, t), at * share, (at + 1) * share)

    def out_copy(g):
        at = pl.ds(GROUP * g, GROUP)
        return pltpu.make_async_copy(out.at[at], out_hbm.at[at], out_sem.at[g])

    def gather_tile(g, t):
        at = pl.ds(pl.multiple_of(t * tile, tile), tile)

        def arrived(source):
            pltpu.make_async_remote_copy(
                src_ref=other.at[0, 0], dst_ref=parts.at[source, g, t], send_sem=swap_send.at[0],
                recv_sem=part_recv.at[source, g, t], device_id={"cand": sibling}, device_id_type=MESH,
            ).wait_recv()

        @pl.when(lax.div(t, here_tiles) != core)
        def _():
            arrived(tp_me)

        for k in range(1, tp_n):
            arrived(lax.rem(tp_me + k, tp_n))
        total = parts[0, g, t].astype(jnp.float32)
        for k in range(1, tp_n):
            total = total + parts[k, g, t].astype(jnp.float32)
        for i in range(GROUP):
            mixed = hidden[GROUP * g + i, :, at].astype(jnp.float32) + total[i * steps:(i + 1) * steps]
            out[GROUP * g + i, :, at] = mixed.astype(jnp.bfloat16)

    def gather(g):
        if g == 0:
            hidden_copy.wait()

        def both_halves(t):
            gather_tile(g, t)
            gather_tile(g, t + here_tiles)

        loop(both_halves, 0, here_tiles)
        out_copy(g).start()

    fork_at = span + 1
    project_at = fork_at + 2
    gather_at = project_at + turns + 3

    def within(at, length):
        return jnp.logical_and(at >= 0, at < length)

    def advance(i):
        @pl.when(i < chunks)
        def _():
            turn(i)

        for p in range(early, problems):
            @pl.when(i == p - early)
            def _(p=p):
                local_part(p)

        @pl.when(jnp.logical_and(outer[1], within(i - LAG_IN, chunks)))
        def _():
            finish(i - LAG_IN)

        now = i - LAG_OUT

        @pl.when(jnp.logical_and(jnp.logical_not(outer[1]), within(now, chunks)))
        def _():
            finish(now)

        for g in range(groups):
            at = now - g * span

            @pl.when(at == fork_at)
            def _(g=g):
                fork_group(g)

            @pl.when(within(at - project_at, turns))
            def _(g=g, at=at):
                project_piece(g, at - project_at)

            @pl.when(at == gather_at)
            def _(g=g):
                gather(g)

    loop(advance, 0, LAG_OUT + gather_at + (groups - 1) * span + 1)

    def rest(j):
        sibling_copy(j).wait_send()
        drain0(j)
        drain1(j)
        fork_copy(j).wait_send()

    loop(rest, 0, chunks)

    def rest_group(g):
        swap_copy(g).wait_send()

        def rest_parts(t):
            other_copy(g, t, 0).wait_send()
            for k in range(1, tp_n):
                part_copy(g, t, k).wait_send()
                other_copy(g, t, k).wait_send()

        loop(rest_parts, 0, here_tiles)
        out_copy(g).wait()

    loop(rest_group, 0, groups)


def local(cand_n, tp_n, hidden_in, queries, new_kv, kv_cache, lengths, winner, out_values, out_scales):
    problems, kv_here, _, slots, head_dim = kv_cache.shape
    steps, heads = queries.shape[1:3]
    depth, width = out_values.shape
    groups = problems // GROUP
    rows = GROUP * steps
    split = 4 if kv_here % 4 == 0 else 1
    hs = kv_here // split
    chunks = problems // PAIR * split
    tile = 512
    tiles = width // tile
    flat = queries.reshape(problems, steps * heads, head_dim)
    fresh = new_kv.reshape(problems, steps * kv_here * 2, head_dim)
    smem = pl.BlockSpec(memory_space=pltpu.SMEM)
    hbm = pl.BlockSpec(memory_space=pl.ANY)
    line = pltpu.VMEM((chunks, hs, 2, BLOCK, head_dim), jnp.bfloat16)
    none = pltpu.VMEM((1, hs, 2, BLOCK, head_dim), jnp.bfloat16)
    short = cand_n // 2 // 4 == 2
    spare = none if short else line
    every = pltpu.VMEM((problems * split, hs, 2, BLOCK, head_dim), jnp.bfloat16)
    stat = pltpu.VMEM((problems, steps * heads, head_dim), jnp.float32)
    dma = pltpu.SemaphoreType.DMA
    return pl.pallas_call(
        functools.partial(kernel, cand_n, tp_n, tile, split),
        out_shape=jax.ShapeDtypeStruct(hidden_in.shape, jnp.bfloat16),
        in_specs=[smem, smem, smem, hbm, hbm, hbm, hbm, hbm],
        out_specs=hbm,
        scratch_shapes=[
            [pltpu.VMEM(kv_cache.shape[1:], jnp.bfloat16)] * problems,
            pltpu.VMEM((depth, width // 2), jnp.bfloat16),
            pltpu.VMEM(flat.shape, jnp.bfloat16),
            pltpu.VMEM(fresh.shape, jnp.bfloat16),
            pltpu.VMEM(hidden_in.shape, jnp.bfloat16),
            pltpu.VMEM(hidden_in.shape, jnp.bfloat16),
            every, line, line,
            spare, spare, line, spare,
            *[line] * 5,
            every, stat, stat, stat,
            pltpu.VMEM((GROUP * steps * heads, head_dim), jnp.float32),
            pltpu.VMEM((2, groups, heads // 2, 2 * rows, 2 * head_dim), jnp.bfloat16),
            pltpu.VMEM((tp_n, groups, tiles, rows, tile), jnp.bfloat16),
            pltpu.VMEM((groups, tiles // 2, rows, tile), jnp.bfloat16),
            dma((problems,)), dma((8,)), dma((3,)), dma((groups,)), dma((8, chunks)), dma((8, chunks)),
            dma((max(tp_n - 1, 1), groups, tiles // 2)), dma((tp_n, groups, tiles)),
            dma((groups,)), dma((groups,)), dma((tp_n, groups, tiles // 2)),
        ],
        compiler_params=pltpu.CompilerParams(
            collective_id=0, has_side_effects=True, vmem_limit_bytes=67043328 - (2 << 20)
        ),
    )(lengths, winner, out_scales, flat, fresh, hidden_in, kv_cache, out_values)


def solution(mesh):
    placed = (
        P("cand", None, None),
        P("cand", None, "tp", None),
        P("cand", None, "tp", None, None),
        P("cand", "tp", None, None, None),
        P("cand"),
        P(),
        P("tp", None),
        P("tp", None),
    )
    return jax.shard_map(
        functools.partial(local, mesh.shape["cand"], mesh.shape["tp"]),
        mesh=mesh, in_specs=placed, out_specs=P("cand", None, None), check_vma=False,
    )
```

```python
import functools
import math

import jax
import jax.numpy as jnp
from jax import lax
from jax.experimental import pallas as pl
from jax.experimental.pallas import tpu as pltpu
from jax.sharding import PartitionSpec as P

BLOCK = 64
LAG_IN = 3
LAG_OUT = 8
PAIR = 2
GROUP = 4
UNIT = 4
LOW = -1e30
MESH = pl.DeviceIdType.MESH


def kernel(
    cand_n, tp_n, tile, split,
    lengths, winner, scales, queries_hbm, fresh_hbm, hidden_hbm, cache_hbm, weights_hbm, out_hbm,
    caches, weights, queries, fresh, hidden, out, blocks, got, own,
    near0, up0, far0, down0, mid, near1, up1, far1, down1,
    fork, top_s, sum_s, acc_s, att, lhs, parts, other,
    cache_sem, weight_sem, small_sem, out_sem, send_sem, recv_sem,
    part_send, part_recv, swap_send, swap_recv, other_send,
):
    me = lax.axis_index("cand")
    tp_me = lax.axis_index("tp")
    problems = len(caches)
    kv_here, _, slots, head_dim = caches[0].shape
    steps_heads = queries.shape[1]
    strips, depth, lanes = weights.shape
    heads = depth // head_dim
    steps = steps_heads // heads
    group = heads // kv_here
    groups = problems // GROUP
    rows = GROUP * steps
    chunks = problems // PAIR * split
    span = GROUP // PAIR * split
    core = lax.rem(me, 2)
    chip = lax.div(me, 2)
    outer_len = 4
    inner_len = cand_n // 2 // outer_len
    inner_at = lax.rem(chip, inner_len)
    outer_at = lax.div(chip, inner_len)
    sibling = me + 1 - 2 * core

    def ends(at, length, stride):
        low_side = at < length // 2
        step = jnp.where(low_side, stride, -stride)
        has_near = jnp.logical_and(at > 0, at < length - 1)
        crosses = jnp.logical_or(at == length // 2 - 1, at == length // 2)
        return length, has_near, crosses, me + step, me - step

    inner = ends(inner_at, inner_len, 2)
    outer = ends(outer_at, outer_len, 2 * inner_len)

    def cache_copy(p):
        return pltpu.make_async_copy(cache_hbm.at[p], caches[p], cache_sem.at[p])

    def weight_copy(i):
        columns = pl.ds(pl.multiple_of((core * strips + i) * lanes, lanes), lanes)
        return pltpu.make_async_copy(weights_hbm.at[:, columns], weights.at[i], weight_sem.at[i])

    queries_copy = pltpu.make_async_copy(queries_hbm, queries, small_sem.at[0])
    fresh_copy = pltpu.make_async_copy(fresh_hbm, fresh, small_sem.at[1])
    hidden_copy = pltpu.make_async_copy(hidden_hbm, hidden, small_sem.at[2])

    for p in range(PAIR):
        cache_copy(p).start()
    queries_copy.start()
    fresh_copy.start()
    for p in range(PAIR, problems):
        cache_copy(p).start()

    barrier = pltpu.get_barrier_semaphore()

    def greet(**where):
        pl.semaphore_signal(barrier, inc=1, device_id=where, device_id_type=MESH)

    greet(cand=sibling)
    count = 1 + 2 * (tp_n - 1)
    for _, has_near, _, far, near in (inner, outer):
        greet(cand=far)

        @pl.when(has_near)
        def _(near=near):
            greet(cand=near)

        count = count + 1 + has_near.astype(jnp.int32)
    for k in range(1, tp_n):
        greet(tp=lax.rem(tp_me + k, tp_n))
        greet(cand=sibling, tp=lax.rem(tp_me + k, tp_n))

    def remote(src, dst, kind, j, target):
        return pltpu.make_async_remote_copy(
            src_ref=src, dst_ref=dst, send_sem=send_sem.at[kind, j],
            recv_sem=recv_sem.at[kind, j], device_id={"cand": target}, device_id_type=MESH,
        )

    def place(side, j):
        return (PAIR * lax.div(j, split) + side) * split + lax.rem(j, split)

    def sibling_copy(j):
        return remote(blocks.at[place(1 - core, j)], got.at[j], 0, j, sibling)

    def loop(body, first, last):
        def step(j, carry):
            body(j)
            return carry

        lax.fori_loop(first, last, step, 0)

    def make_line(line, kind, base_ref, near_ref, up_ref, far_ref, down_ref):
        length, has_near, crosses, far_id, near_id = line
        short = length == 2
        if short:
            up_ref = base_ref

        def to_far_in(j):
            return remote(up_ref.at[j], near_ref.at[j], kind, j, far_id)

        def to_far_cross(j):
            return remote(up_ref.at[j], far_ref.at[j], kind + 1, j, far_id)

        def to_near(j):
            return pltpu.make_async_remote_copy(
                src_ref=down_ref.at[j], dst_ref=far_ref.at[j], send_sem=send_sem.at[kind + 2, j],
                recv_sem=recv_sem.at[kind + 1, j], device_id={"cand": near_id}, device_id_type=MESH,
            )

        def climb(j):
            if short:
                to_far_cross(j).start()
                return

            @pl.when(has_near)
            def _():
                to_far_in(j).wait_recv()
                up_ref[j] = base_ref[j] + near_ref[j]

            @pl.when(jnp.logical_not(has_near))
            def _():
                up_ref[j] = base_ref[j]

            @pl.when(crosses)
            def _():
                to_far_cross(j).start()

            @pl.when(jnp.logical_not(crosses))
            def _():
                to_far_in(j).start()

        def settle(j):
            to_far_cross(j).wait_recv()
            if not short:
                @pl.when(has_near)
                def _():
                    down_ref[j] = base_ref[j] + far_ref[j]
                    to_near(j).start()

            return up_ref[j] + far_ref[j]

        def drain(j):
            if short:
                to_far_cross(j).wait_send()
                return

            @pl.when(crosses)
            def _():
                to_far_cross(j).wait_send()

            @pl.when(jnp.logical_not(crosses))
            def _():
                to_far_in(j).wait_send()

            @pl.when(has_near)
            def _():
                to_near(j).wait_send()

        return climb, settle, drain

    climb0, settle0, drain0 = make_line(inner, 1, own, near0, up0, far0, down0)
    climb1, settle1, drain1 = make_line(outer, 4, mid, near1, up1, far1, down1)

    def enter(j):
        sibling_copy(j).wait_recv()
        own[j] = blocks[place(core, j)] + got[j]
        climb0(j)

    factor = 1.0 / math.sqrt(head_dim)

    def row_of(width):
        return lax.broadcasted_iota(jnp.int32, (steps_heads, width), 0)

    def col_of(width):
        return lax.broadcasted_iota(jnp.int32, (steps_heads, width), 1)

    def score(q, keys):
        return lax.dot_general(q, keys, (((1,), (1,)), ((), ())), preferred_element_type=jnp.float32) * factor

    pick_row = lax.broadcasted_iota(jnp.int32, (BLOCK, slots), 0)
    pick_col = lax.broadcasted_iota(jnp.int32, (BLOCK, slots), 1)
    unit = blocks.shape[1]

    def pick(p):
        hit = jnp.logical_and(
            pick_col - pick_row == lengths[p] - BLOCK, jnp.zeros_like(pick_col) + winner[p] == me
        )
        chosen = hit.astype(jnp.float32).astype(jnp.bfloat16)
        for h in range(kv_here):
            for kv in range(2):
                at = p * kv_here * 2 + h * 2 + kv
                blocks[at // unit, at % unit] = jnp.dot(
                    chosen, caches[p][h, kv], preferred_element_type=jnp.float32
                ).astype(jnp.bfloat16)

    def local_part(p):
        q = queries[p]
        s = score(q, caches[p][:, 0].reshape(kv_here * slots, head_dim))
        row, col = row_of(kv_here * slots), col_of(kv_here * slots)
        mine = lax.div(lax.rem(row, heads), group) == lax.div(col, slots)
        s = jnp.where(jnp.logical_and(mine, lax.rem(col, slots) < lengths[p] - BLOCK), s, LOW)
        both = fresh[p]
        n = score(q, both)
        width = both.shape[0]
        row, col = row_of(width), col_of(width)
        mine = lax.div(lax.rem(row, heads), group) == lax.rem(lax.div(col, 2), kv_here)
        mine = jnp.logical_and(mine, lax.rem(col, 2) == 0)
        n = jnp.where(jnp.logical_and(mine, lax.div(col, 2 * kv_here) <= lax.div(row, heads)), n, LOW)
        wide = both.astype(jnp.float32)
        values = jnp.concatenate([wide[1:], wide[:1]], 0).astype(jnp.bfloat16)
        top = jnp.maximum(jnp.max(s, 1, keepdims=True), jnp.max(n, 1, keepdims=True))
        s = jnp.exp(s - top)
        n = jnp.exp(n - top)
        top_s[p] = jnp.broadcast_to(top, (steps_heads, head_dim))
        sum_s[p] = jnp.broadcast_to(jnp.sum(s, 1, keepdims=True) + jnp.sum(n, 1, keepdims=True), (steps_heads, head_dim))
        acc_s[p] = jnp.dot(
            s.astype(jnp.bfloat16), caches[p][:, 1].reshape(kv_here * slots, head_dim),
            preferred_element_type=jnp.float32,
        ) + jnp.dot(n.astype(jnp.bfloat16), values, preferred_element_type=jnp.float32)

    for g in range(problems // PAIR):
        for p in range(PAIR * g, PAIR * (g + 1)):
            cache_copy(p).wait()
            pick(p)
        if g == 0:
            pl.semaphore_wait(barrier, count)
        loop(lambda j: sibling_copy(j).start(), g * split, (g + 1) * split)
        if g > 0:
            loop(enter, (g - 1) * split, g * split)
    loop(lambda i: weight_copy(i).start(), 0, strips)
    hidden_copy.start()
    queries_copy.wait()
    fresh_copy.wait()
    early = problems // 2
    local_part(0)
    loop(enter, chunks - split, chunks)
    for p in range(1, early):
        local_part(p)

    def turn(j):
        mid[j] = settle0(j)
        climb1(j)

    def fork_copy(j):
        at = place(core, j)
        return remote(fork.at[at], fork.at[at], 7, j, sibling)

    def finish(j):
        fork[place(core, j)] = settle1(j)
        fork_copy(j).start()

    def closing(j):
        remote(got.at[j], fork.at[place(1 - core, j)], 7, j, sibling).wait_recv()

    def fork_part(p, slot):
        q = queries[p]
        both = fork[pl.ds(p * split, split)].reshape(kv_here, 2, BLOCK, head_dim)
        keys = both[:, 0].reshape(kv_here * BLOCK, head_dim)
        values = both[:, 1].reshape(kv_here * BLOCK, head_dim)
        s = score(q, keys)
        row, col = row_of(kv_here * BLOCK), col_of(kv_here * BLOCK)
        mine = lax.div(lax.rem(row, heads), group) == lax.div(col, BLOCK)
        s = jnp.where(mine, s, LOW)
        before = top_s[p]
        top = jnp.maximum(before, jnp.max(s, 1, keepdims=True))
        s = jnp.exp(s - top[:, :1])
        scale = jnp.exp(before - top)
        total = sum_s[p] * scale + jnp.sum(s, 1, keepdims=True)
        acc = acc_s[p] * scale + jnp.dot(s.astype(jnp.bfloat16), values, preferred_element_type=jnp.float32)
        att[pl.ds(slot * steps_heads, steps_heads), :] = acc / total

    pairs = heads // 2

    def swap_copy(g):
        return pltpu.make_async_remote_copy(
            src_ref=lhs.at[0, g], dst_ref=lhs.at[1, g], send_sem=swap_send.at[g], recv_sem=swap_recv.at[g],
            device_id={"cand": sibling}, device_id_type=MESH,
        )

    def fork_group(g):
        loop(closing, g * span, (g + 1) * span)
        loop(lambda i: fork_part(GROUP * g + i, i), 0, GROUP)
        empty = jnp.zeros((rows, head_dim), jnp.float32)
        for i in range(pairs):
            a = att[pl.ds(2 * i, rows, stride=heads), :]
            b = att[pl.ds(2 * i + 1, rows, stride=heads), :]
            lhs[0, g, i] = jnp.concatenate(
                [jnp.concatenate([a, empty], 1), jnp.concatenate([empty, b], 1)], 0
            ).astype(jnp.bfloat16)
        swap_copy(g).start()

    tiles = parts.shape[2]
    here_tiles = tiles // 2
    per = tile // head_dim

    def part_copy(g, t, k):
        at = core * here_tiles + t
        return pltpu.make_async_remote_copy(
            src_ref=parts.at[tp_me, g, at], dst_ref=parts.at[tp_me, g, at], send_sem=part_send.at[k - 1, g, t],
            recv_sem=part_recv.at[tp_me, g, at], device_id={"tp": lax.rem(tp_me + k, tp_n)},
            device_id_type=MESH,
        )

    def other_copy(g, t, k):
        at = core * here_tiles + t
        return pltpu.make_async_remote_copy(
            src_ref=other.at[g, t], dst_ref=parts.at[tp_me, g, at], send_sem=other_send.at[k, g, t],
            recv_sem=part_recv.at[tp_me, g, at],
            device_id={"cand": sibling, "tp": lax.rem(tp_me + k, tp_n)}, device_id_type=MESH,
        )

    def project(g, t):
        first_scale = (core * here_tiles + t) * per
        row = lax.broadcasted_iota(jnp.int32, (4 * rows, head_dim), 0)
        even = lax.rem(row, 2 * rows) < rows
        total = [jnp.zeros((4 * rows, head_dim), jnp.float32) for _ in range(per)]
        for i in range(pairs):
            block = [weights[t * per + c, pl.ds(2 * i * head_dim, 2 * head_dim)] for c in range(per)]
            product = jnp.dot(
                lhs[:, g, i].reshape(4 * rows, 2 * head_dim), jnp.concatenate(block, 1),
                preferred_element_type=jnp.float32,
            )
            for c in range(per):
                scale = jnp.where(even, scales[2 * i, first_scale + c], scales[2 * i + 1, first_scale + c])
                total[c] = total[c] + product[:, c * head_dim:(c + 1) * head_dim] * scale
        whole = jnp.concatenate(total, 1).reshape(2, 2, rows, tile)
        whole = (whole[:, 0] + whole[:, 1]).astype(jnp.bfloat16)
        parts[tp_me, g, core * here_tiles + t] = whole[0]
        other[g, t] = whole[1]
        for k in range(1, tp_n):
            other_copy(g, t, k).start()
            part_copy(g, t, k).start()
        other_copy(g, t, 0).start()

    share = max(here_tiles // span, 1)
    turns = here_tiles // share

    def project_piece(g, at):
        @pl.when(at == 0)
        def _():
            swap_copy(g).wait_recv()

        def one(t):
            if g == 0:
                for c in range(per):
                    weight_copy(t * per + c).wait()
            project(g, t)

        loop(one, at * share, (at + 1) * share)

    def out_copy(g):
        at = pl.ds(GROUP * g, GROUP)
        return pltpu.make_async_copy(out.at[at], out_hbm.at[at], out_sem.at[g])

    def gather_tile(g, t):
        at = pl.ds(pl.multiple_of(t * tile, tile), tile)

        def arrived(source):
            pltpu.make_async_remote_copy(
                src_ref=other.at[0, 0], dst_ref=parts.at[source, g, t], send_sem=swap_send.at[0],
                recv_sem=part_recv.at[source, g, t], device_id={"cand": sibling}, device_id_type=MESH,
            ).wait_recv()

        @pl.when(lax.div(t, here_tiles) != core)
        def _():
            arrived(tp_me)

        for k in range(1, tp_n):
            arrived(lax.rem(tp_me + k, tp_n))
        total = parts[0, g, t].astype(jnp.float32)
        for k in range(1, tp_n):
            total = total + parts[k, g, t].astype(jnp.float32)
        for i in range(GROUP):
            mixed = hidden[GROUP * g + i, :, at].astype(jnp.float32) + total[i * steps:(i + 1) * steps]
            out[GROUP * g + i, :, at] = mixed.astype(jnp.bfloat16)

    def gather(g):
        if g == 0:
            hidden_copy.wait()

        def both_halves(t):
            gather_tile(g, t)
            gather_tile(g, t + here_tiles)

        loop(both_halves, 0, here_tiles)
        out_copy(g).start()

    fork_at = span
    project_at = fork_at + 1
    gather_at = project_at + turns

    def within(at, length):
        return jnp.logical_and(at >= 0, at < length)

    def advance(i):
        @pl.when(i < chunks)
        def _():
            turn(i)

        for p in range(early, problems):
            @pl.when(i == p - early)
            def _(p=p):
                local_part(p)

        @pl.when(jnp.logical_and(outer[1], within(i - LAG_IN, chunks)))
        def _():
            finish(i - LAG_IN)

        now = i - LAG_OUT

        for g in range(groups):
            at = now - g * span

            @pl.when(at == gather_at)
            def _(g=g):
                gather(g)

        for g in range(groups):
            at = now - g * span

            @pl.when(within(at - project_at, turns))
            def _(g=g, at=at):
                project_piece(g, at - project_at)

        for g in range(groups):
            @pl.when(now - g * span == fork_at)
            def _(g=g):
                fork_group(g)

        @pl.when(jnp.logical_and(jnp.logical_not(outer[1]), within(now, chunks)))
        def _():
            finish(now)

    loop(advance, 0, LAG_OUT + gather_at + (groups - 1) * span + 1)

    def rest(j):
        sibling_copy(j).wait_send()
        drain0(j)
        drain1(j)
        fork_copy(j).wait_send()

    loop(rest, 0, chunks)

    def rest_group(g):
        swap_copy(g).wait_send()

        def rest_parts(t):
            other_copy(g, t, 0).wait_send()
            for k in range(1, tp_n):
                part_copy(g, t, k).wait_send()
                other_copy(g, t, k).wait_send()

        loop(rest_parts, 0, here_tiles)
        out_copy(g).wait()

    loop(rest_group, 0, groups)


def local(cand_n, tp_n, hidden_in, queries, new_kv, kv_cache, lengths, winner, out_values, out_scales):
    problems, kv_here, _, slots, head_dim = kv_cache.shape
    steps, heads = queries.shape[1:3]
    depth, width = out_values.shape
    groups = problems // GROUP
    rows = GROUP * steps
    unit = min(UNIT, kv_here * 2)
    split = kv_here * 2 // unit
    chunks = problems // PAIR * split
    tile = 1024
    tiles = width // tile
    strips = width // 2 // 128
    flat = queries.reshape(problems, steps * heads, head_dim)
    fresh = new_kv.reshape(problems, steps * kv_here * 2, head_dim)
    smem = pl.BlockSpec(memory_space=pltpu.SMEM)
    hbm = pl.BlockSpec(memory_space=pl.ANY)
    line = pltpu.VMEM((chunks, unit, BLOCK, head_dim), jnp.bfloat16)
    none = pltpu.VMEM((1, unit, BLOCK, head_dim), jnp.bfloat16)
    short = cand_n // 2 // 4 == 2
    spare = none if short else line
    every = pltpu.VMEM((problems * split, unit, BLOCK, head_dim), jnp.bfloat16)
    stat = pltpu.VMEM((problems, steps * heads, head_dim), jnp.float32)
    dma = pltpu.SemaphoreType.DMA
    return pl.pallas_call(
        functools.partial(kernel, cand_n, tp_n, tile, split),
        out_shape=jax.ShapeDtypeStruct(hidden_in.shape, jnp.bfloat16),
        in_specs=[smem, smem, smem, hbm, hbm, hbm, hbm, hbm],
        out_specs=hbm,
        scratch_shapes=[
            [pltpu.VMEM(kv_cache.shape[1:], jnp.bfloat16)] * problems,
            pltpu.VMEM((strips, depth, 128), jnp.bfloat16),
            pltpu.VMEM(flat.shape, jnp.bfloat16),
            pltpu.VMEM(fresh.shape, jnp.bfloat16),
            pltpu.VMEM(hidden_in.shape, jnp.bfloat16),
            pltpu.VMEM(hidden_in.shape, jnp.bfloat16),
            every, line, line,
            spare, spare, line, spare,
            *[line] * 5,
            every, stat, stat, stat,
            pltpu.VMEM((GROUP * steps * heads, head_dim), jnp.float32),
            pltpu.VMEM((2, groups, heads // 2, 2 * rows, 2 * head_dim), jnp.bfloat16),
            pltpu.VMEM((tp_n, groups, tiles, rows, tile), jnp.bfloat16),
            pltpu.VMEM((groups, tiles // 2, rows, tile), jnp.bfloat16),
            dma((problems,)), dma((strips,)), dma((3,)), dma((groups,)), dma((8, chunks)), dma((8, chunks)),
            dma((max(tp_n - 1, 1), groups, tiles // 2)), dma((tp_n, groups, tiles)),
            dma((groups,)), dma((groups,)), dma((tp_n, groups, tiles // 2)),
        ],
        compiler_params=pltpu.CompilerParams(
            collective_id=0, has_side_effects=True, vmem_limit_bytes=67043328 - (2 << 20)
        ),
    )(lengths, winner, out_scales, flat, fresh, hidden_in, kv_cache, out_values)


def solution(mesh):
    placed = (
        P("cand", None, None),
        P("cand", None, "tp", None),
        P("cand", None, "tp", None, None),
        P("cand", "tp", None, None, None),
        P("cand"),
        P(),
        P("tp", None),
        P("tp", None),
    )
    return jax.shard_map(
        functools.partial(local, mesh.shape["cand"], mesh.shape["tp"]),
        mesh=mesh, in_specs=placed, out_specs=P("cand", None, None), check_vma=False,
    )
```

```python
import functools
import math

import jax
import jax.numpy as jnp
from jax import lax
from jax.experimental import pallas as pl
from jax.experimental.pallas import tpu as pltpu
from jax.sharding import PartitionSpec as P

BLOCK = 64
LAG_IN = 3
LAG_OUT = 8
LAG_X = 3
PAIR = 2
GROUP = 4
UNIT = 4
LOW = -1e30
MESH = pl.DeviceIdType.MESH


def kernel(
    cand_n, tp_n, tile, split,
    lengths, winner, scales, queries_hbm, fresh_hbm, hidden_hbm, cache_hbm, weights_hbm, out_hbm,
    caches, weights, queries, fresh, hidden, out, blocks, got, own,
    near0, up0, far0, down0, mid, near1, up1, far1, down1,
    fork, top_s, sum_s, acc_s, att, lhs, parts, other,
    cache_sem, weight_sem, small_sem, out_sem, send_sem, recv_sem,
    part_send, part_recv, swap_send, swap_recv, other_send,
):
    me = lax.axis_index("cand")
    tp_me = lax.axis_index("tp")
    problems = len(caches)
    kv_here, _, slots, head_dim = caches[0].shape
    steps_heads = queries.shape[1]
    strips, depth, lanes = weights.shape
    heads = depth // head_dim
    steps = steps_heads // heads
    group = heads // kv_here
    groups = problems // GROUP
    rows = GROUP * steps
    chunks = problems // PAIR * split
    span = GROUP // PAIR * split
    core = lax.rem(me, 2)
    chip = lax.div(me, 2)
    outer_len = 4
    inner_len = cand_n // 2 // outer_len
    inner_at = lax.rem(chip, inner_len)
    outer_at = lax.div(chip, inner_len)
    sibling = me + 1 - 2 * core

    def ends(at, length, stride):
        low_side = at < length // 2
        step = jnp.where(low_side, stride, -stride)
        has_near = jnp.logical_and(at > 0, at < length - 1)
        crosses = jnp.logical_or(at == length // 2 - 1, at == length // 2)
        return has_near, crosses, me + step, me - step

    inner = ends(inner_at, inner_len, 2)
    outer = ends(outer_at, outer_len, 2 * inner_len)

    def cache_copy(p):
        return pltpu.make_async_copy(cache_hbm.at[p], caches[p], cache_sem.at[p])

    def weight_copy(i):
        columns = pl.ds(pl.multiple_of((core * strips + i) * lanes, lanes), lanes)
        return pltpu.make_async_copy(weights_hbm.at[:, columns], weights.at[i], weight_sem.at[i])

    queries_copy = pltpu.make_async_copy(queries_hbm, queries, small_sem.at[0])
    fresh_copy = pltpu.make_async_copy(fresh_hbm, fresh, small_sem.at[1])
    hidden_copy = pltpu.make_async_copy(hidden_hbm, hidden, small_sem.at[2])

    for p in range(PAIR):
        cache_copy(p).start()
    queries_copy.start()
    fresh_copy.start()
    for p in range(PAIR, problems):
        cache_copy(p).start()

    barrier = pltpu.get_barrier_semaphore()

    def greet(**where):
        pl.semaphore_signal(barrier, inc=1, device_id=where, device_id_type=MESH)

    greet(cand=sibling)
    count = 1 + 2 * (tp_n - 1)
    for has_near, _, far, near in (inner, outer):
        greet(cand=far)

        @pl.when(has_near)
        def _(near=near):
            greet(cand=near)

        count = count + 1 + has_near.astype(jnp.int32)
    for k in range(1, tp_n):
        greet(tp=lax.rem(tp_me + k, tp_n))
        greet(cand=sibling, tp=lax.rem(tp_me + k, tp_n))

    def remote(src, dst, kind, j, target):
        return pltpu.make_async_remote_copy(
            src_ref=src, dst_ref=dst, send_sem=send_sem.at[kind, j],
            recv_sem=recv_sem.at[kind, j], device_id={"cand": target}, device_id_type=MESH,
        )

    def place(side, j):
        return (PAIR * lax.div(j, split) + side) * split + lax.rem(j, split)

    def sibling_copy(j):
        return remote(blocks.at[place(1 - core, j)], got.at[j], 0, j, sibling)

    def loop(body, first, last):
        def step(j, carry):
            body(j)
            return carry

        lax.fori_loop(first, last, step, 0)

    def make_line(line, kind, base_ref, near_ref, up_ref, far_ref, down_ref):
        has_near, crosses, far_id, near_id = line

        def to_far_in(j):
            return remote(up_ref.at[j], near_ref.at[j], kind, j, far_id)

        def to_far_cross(j):
            return remote(up_ref.at[j], far_ref.at[j], kind + 1, j, far_id)

        def to_near(j):
            return pltpu.make_async_remote_copy(
                src_ref=down_ref.at[j], dst_ref=far_ref.at[j], send_sem=send_sem.at[kind + 2, j],
                recv_sem=recv_sem.at[kind + 1, j], device_id={"cand": near_id}, device_id_type=MESH,
            )

        def climb(j):
            @pl.when(has_near)
            def _():
                to_far_in(j).wait_recv()
                up_ref[j] = base_ref[j] + near_ref[j]

            @pl.when(jnp.logical_not(has_near))
            def _():
                up_ref[j] = base_ref[j]

            @pl.when(crosses)
            def _():
                to_far_cross(j).start()

            @pl.when(jnp.logical_not(crosses))
            def _():
                to_far_in(j).start()

        def settle(j):
            to_far_cross(j).wait_recv()

            @pl.when(has_near)
            def _():
                down_ref[j] = base_ref[j] + far_ref[j]
                to_near(j).start()

            return up_ref[j] + far_ref[j]

        def drain(j):
            @pl.when(crosses)
            def _():
                to_far_cross(j).wait_send()

            @pl.when(jnp.logical_not(crosses))
            def _():
                to_far_in(j).wait_send()

            @pl.when(has_near)
            def _():
                to_near(j).wait_send()

        return climb, settle, drain

    def choose(a, b):
        return (
            *[jnp.logical_or(jnp.logical_and(core == 0, p), jnp.logical_and(core == 1, q)) for p, q in zip(a[:2], b[:2])],
            *[jnp.where(core == 0, p, q) for p, q in zip(a[2:], b[2:])],
        )

    first = choose(inner, outer)
    second = choose(outer, inner)
    eager = jnp.logical_not(first[0])
    climb0, settle0, drain0 = make_line(first, 1, own, near0, up0, far0, down0)
    climb1, settle1, drain1 = make_line(second, 4, mid, near1, up1, far1, down1)

    def enter(j):
        sibling_copy(j).wait_recv()
        own[j] = blocks[place(core, j)] + got[j]
        climb0(j)

    factor = 1.0 / math.sqrt(head_dim)

    def row_of(width):
        return lax.broadcasted_iota(jnp.int32, (steps_heads, width), 0)

    def col_of(width):
        return lax.broadcasted_iota(jnp.int32, (steps_heads, width), 1)

    def score(q, keys):
        return lax.dot_general(q, keys, (((1,), (1,)), ((), ())), preferred_element_type=jnp.float32) * factor

    pick_row = lax.broadcasted_iota(jnp.int32, (BLOCK, slots), 0)
    pick_col = lax.broadcasted_iota(jnp.int32, (BLOCK, slots), 1)
    unit = blocks.shape[1]

    def pick(p):
        hit = jnp.logical_and(
            pick_col - pick_row == lengths[p] - BLOCK, jnp.zeros_like(pick_col) + winner[p] == me
        )
        chosen = hit.astype(jnp.float32).astype(jnp.bfloat16)
        for h in range(kv_here):
            for kv in range(2):
                at = p * kv_here * 2 + h * 2 + kv
                blocks[at // unit, at % unit] = jnp.dot(
                    chosen, caches[p][h, kv], preferred_element_type=jnp.float32
                ).astype(jnp.bfloat16)

    def local_part(p):
        q = queries[p]
        s = score(q, caches[p][:, 0].reshape(kv_here * slots, head_dim))
        row, col = row_of(kv_here * slots), col_of(kv_here * slots)
        mine = lax.div(lax.rem(row, heads), group) == lax.div(col, slots)
        s = jnp.where(jnp.logical_and(mine, lax.rem(col, slots) < lengths[p] - BLOCK), s, LOW)
        both = fresh[p]
        n = score(q, both)
        width = both.shape[0]
        row, col = row_of(width), col_of(width)
        mine = lax.div(lax.rem(row, heads), group) == lax.rem(lax.div(col, 2), kv_here)
        mine = jnp.logical_and(mine, lax.rem(col, 2) == 0)
        n = jnp.where(jnp.logical_and(mine, lax.div(col, 2 * kv_here) <= lax.div(row, heads)), n, LOW)
        wide = both.astype(jnp.float32)
        values = jnp.concatenate([wide[1:], wide[:1]], 0).astype(jnp.bfloat16)
        top = jnp.maximum(jnp.max(s, 1, keepdims=True), jnp.max(n, 1, keepdims=True))
        s = jnp.exp(s - top)
        n = jnp.exp(n - top)
        top_s[p] = jnp.broadcast_to(top, (steps_heads, head_dim))
        sum_s[p] = jnp.broadcast_to(jnp.sum(s, 1, keepdims=True) + jnp.sum(n, 1, keepdims=True), (steps_heads, head_dim))
        acc_s[p] = jnp.dot(
            s.astype(jnp.bfloat16), caches[p][:, 1].reshape(kv_here * slots, head_dim),
            preferred_element_type=jnp.float32,
        ) + jnp.dot(n.astype(jnp.bfloat16), values, preferred_element_type=jnp.float32)

    for g in range(problems // PAIR):
        for p in range(PAIR * g, PAIR * (g + 1)):
            cache_copy(p).wait()
            pick(p)
        if g == 0:
            pl.semaphore_wait(barrier, count)
        loop(lambda j: sibling_copy(j).start(), g * split, (g + 1) * split)
        if g > 0:
            @pl.when(eager)
            def _(g=g):
                loop(enter, (g - 1) * split, g * split)

    loop(lambda i: weight_copy(i).start(), 0, strips)
    hidden_copy.start()
    queries_copy.wait()
    fresh_copy.wait()
    early = problems // 2
    local_part(0)

    @pl.when(eager)
    def _():
        loop(enter, chunks - split, chunks)

    for p in range(1, early):
        local_part(p)

    def turn(j):
        mid[j] = settle0(j)
        climb1(j)

    def fork_copy(j):
        at = place(core, j)
        return remote(fork.at[at], fork.at[at], 7, j, sibling)

    def finish(j):
        fork[place(core, j)] = settle1(j)
        fork_copy(j).start()

    def closing(j):
        remote(got.at[j], fork.at[place(1 - core, j)], 7, j, sibling).wait_recv()

    def fork_part(p, slot):
        q = queries[p]
        both = fork[pl.ds(p * split, split)].reshape(kv_here, 2, BLOCK, head_dim)
        keys = both[:, 0].reshape(kv_here * BLOCK, head_dim)
        values = both[:, 1].reshape(kv_here * BLOCK, head_dim)
        s = score(q, keys)
        row, col = row_of(kv_here * BLOCK), col_of(kv_here * BLOCK)
        mine = lax.div(lax.rem(row, heads), group) == lax.div(col, BLOCK)
        s = jnp.where(mine, s, LOW)
        before = top_s[p]
        top = jnp.maximum(before, jnp.max(s, 1, keepdims=True))
        s = jnp.exp(s - top[:, :1])
        scale = jnp.exp(before - top)
        total = sum_s[p] * scale + jnp.sum(s, 1, keepdims=True)
        acc = acc_s[p] * scale + jnp.dot(s.astype(jnp.bfloat16), values, preferred_element_type=jnp.float32)
        att[pl.ds(slot * steps_heads, steps_heads), :] = acc / total

    pairs = heads // 2

    def swap_copy(g):
        return pltpu.make_async_remote_copy(
            src_ref=lhs.at[0, g], dst_ref=lhs.at[1, g], send_sem=swap_send.at[g], recv_sem=swap_recv.at[g],
            device_id={"cand": sibling}, device_id_type=MESH,
        )

    def fork_group(g):
        loop(closing, g * span, (g + 1) * span)
        loop(lambda i: fork_part(GROUP * g + i, i), 0, GROUP)
        empty = jnp.zeros((rows, head_dim), jnp.float32)
        for i in range(pairs):
            a = att[pl.ds(2 * i, rows, stride=heads), :]
            b = att[pl.ds(2 * i + 1, rows, stride=heads), :]
            lhs[0, g, i] = jnp.concatenate(
                [jnp.concatenate([a, empty], 1), jnp.concatenate([empty, b], 1)], 0
            ).astype(jnp.bfloat16)
        swap_copy(g).start()

    tiles = parts.shape[2]
    here_tiles = tiles // 2
    per = tile // head_dim

    def part_copy(g, t, k):
        at = core * here_tiles + t
        return pltpu.make_async_remote_copy(
            src_ref=parts.at[tp_me, g, at], dst_ref=parts.at[tp_me, g, at], send_sem=part_send.at[k - 1, g, t],
            recv_sem=part_recv.at[tp_me, g, at], device_id={"tp": lax.rem(tp_me + k, tp_n)},
            device_id_type=MESH,
        )

    def other_copy(g, t, k):
        at = core * here_tiles + t
        return pltpu.make_async_remote_copy(
            src_ref=other.at[g, t], dst_ref=parts.at[tp_me, g, at], send_sem=other_send.at[k, g, t],
            recv_sem=part_recv.at[tp_me, g, at],
            device_id={"cand": sibling, "tp": lax.rem(tp_me + k, tp_n)}, device_id_type=MESH,
        )

    def project(g, t):
        first_scale = (core * here_tiles + t) * per
        row = lax.broadcasted_iota(jnp.int32, (4 * rows, head_dim), 0)
        even = lax.rem(row, 2 * rows) < rows
        total = [jnp.zeros((4 * rows, head_dim), jnp.float32) for _ in range(per)]
        for i in range(pairs):
            block = [weights[t * per + c, pl.ds(2 * i * head_dim, 2 * head_dim)] for c in range(per)]
            product = jnp.dot(
                lhs[:, g, i].reshape(4 * rows, 2 * head_dim), jnp.concatenate(block, 1),
                preferred_element_type=jnp.float32,
            )
            for c in range(per):
                scale = jnp.where(even, scales[2 * i, first_scale + c], scales[2 * i + 1, first_scale + c])
                total[c] = total[c] + product[:, c * head_dim:(c + 1) * head_dim] * scale
        whole = jnp.concatenate(total, 1).reshape(2, 2, rows, tile)
        whole = (whole[:, 0] + whole[:, 1]).astype(jnp.bfloat16)
        parts[tp_me, g, core * here_tiles + t] = whole[0]
        other[g, t] = whole[1]
        for k in range(1, tp_n):
            other_copy(g, t, k).start()
            part_copy(g, t, k).start()
        other_copy(g, t, 0).start()

    share = max(here_tiles // span, 1)
    turns = here_tiles // share

    def project_piece(g, at):
        @pl.when(at == 0)
        def _():
            swap_copy(g).wait_recv()

        def one(t):
            if g == 0:
                for c in range(per):
                    weight_copy(t * per + c).wait()
            project(g, t)

        loop(one, at * share, (at + 1) * share)

    def out_copy(g):
        at = pl.ds(GROUP * g, GROUP)
        return pltpu.make_async_copy(out.at[at], out_hbm.at[at], out_sem.at[g])

    def gather_tile(g, t):
        at = pl.ds(pl.multiple_of(t * tile, tile), tile)

        def arrived(source):
            pltpu.make_async_remote_copy(
                src_ref=other.at[0, 0], dst_ref=parts.at[source, g, t], send_sem=swap_send.at[0],
                recv_sem=part_recv.at[source, g, t], device_id={"cand": sibling}, device_id_type=MESH,
            ).wait_recv()

        @pl.when(lax.div(t, here_tiles) != core)
        def _():
            arrived(tp_me)

        for k in range(1, tp_n):
            arrived(lax.rem(tp_me + k, tp_n))
        total = parts[0, g, t].astype(jnp.float32)
        for k in range(1, tp_n):
            total = total + parts[k, g, t].astype(jnp.float32)
        for i in range(GROUP):
            mixed = hidden[GROUP * g + i, :, at].astype(jnp.float32) + total[i * steps:(i + 1) * steps]
            out[GROUP * g + i, :, at] = mixed.astype(jnp.bfloat16)

    def gather(g):
        if g == 0:
            hidden_copy.wait()

        def both_halves(t):
            gather_tile(g, t)
            gather_tile(g, t + here_tiles)

        loop(both_halves, 0, here_tiles)
        out_copy(g).start()

    fork_at = span
    project_at = fork_at + 1
    gather_at = project_at + turns

    def within(at, length):
        return jnp.logical_and(at >= 0, at < length)

    def advance(i):
        @pl.when(jnp.logical_and(first[0], i < chunks))
        def _():
            enter(i)

        j = i - jnp.where(first[0], LAG_IN, 0)

        @pl.when(within(j, chunks))
        def _():
            turn(j)

        for p in range(early, problems):
            @pl.when(i == p - early)
            def _(p=p):
                local_part(p)

        @pl.when(jnp.logical_and(second[0], within(j - LAG_IN, chunks)))
        def _():
            finish(j - LAG_IN)

        now = j - jnp.where(core == 0, LAG_OUT, LAG_X if inner_len == 2 else LAG_OUT)

        for g in range(groups):
            at = now - g * span

            @pl.when(at == gather_at)
            def _(g=g):
                gather(g)

        for g in range(groups):
            at = now - g * span

            @pl.when(within(at - project_at, turns))
            def _(g=g, at=at):
                project_piece(g, at - project_at)

        for g in range(groups):
            @pl.when(now - g * span == fork_at)
            def _(g=g):
                fork_group(g)

        @pl.when(jnp.logical_and(jnp.logical_not(second[0]), within(now, chunks)))
        def _():
            finish(now)

    loop(advance, 0, LAG_IN + LAG_OUT + gather_at + (groups - 1) * span + 1)

    def rest(j):
        sibling_copy(j).wait_send()
        drain0(j)
        drain1(j)
        fork_copy(j).wait_send()

    loop(rest, 0, chunks)

    def rest_group(g):
        swap_copy(g).wait_send()

        def rest_parts(t):
            other_copy(g, t, 0).wait_send()
            for k in range(1, tp_n):
                part_copy(g, t, k).wait_send()
                other_copy(g, t, k).wait_send()

        loop(rest_parts, 0, here_tiles)
        out_copy(g).wait()

    loop(rest_group, 0, groups)


def local(cand_n, tp_n, hidden_in, queries, new_kv, kv_cache, lengths, winner, out_values, out_scales):
    problems, kv_here, _, slots, head_dim = kv_cache.shape
    steps, heads = queries.shape[1:3]
    depth, width = out_values.shape
    groups = problems // GROUP
    rows = GROUP * steps
    unit = min(UNIT, kv_here * 2)
    split = kv_here * 2 // unit
    chunks = problems // PAIR * split
    tile = 1024
    tiles = width // tile
    strips = width // 2 // 128
    flat = queries.reshape(problems, steps * heads, head_dim)
    fresh = new_kv.reshape(problems, steps * kv_here * 2, head_dim)
    smem = pl.BlockSpec(memory_space=pltpu.SMEM)
    hbm = pl.BlockSpec(memory_space=pl.ANY)
    line = pltpu.VMEM((chunks, unit, BLOCK, head_dim), jnp.bfloat16)
    every = pltpu.VMEM((problems * split, unit, BLOCK, head_dim), jnp.bfloat16)
    stat = pltpu.VMEM((problems, steps * heads, head_dim), jnp.float32)
    dma = pltpu.SemaphoreType.DMA
    return pl.pallas_call(
        functools.partial(kernel, cand_n, tp_n, tile, split),
        out_shape=jax.ShapeDtypeStruct(hidden_in.shape, jnp.bfloat16),
        in_specs=[smem, smem, smem, hbm, hbm, hbm, hbm, hbm],
        out_specs=hbm,
        scratch_shapes=[
            [pltpu.VMEM(kv_cache.shape[1:], jnp.bfloat16)] * problems,
            pltpu.VMEM((strips, depth, 128), jnp.bfloat16),
            pltpu.VMEM(flat.shape, jnp.bfloat16),
            pltpu.VMEM(fresh.shape, jnp.bfloat16),
            pltpu.VMEM(hidden_in.shape, jnp.bfloat16),
            pltpu.VMEM(hidden_in.shape, jnp.bfloat16),
            every, line, line,
            *[line] * 9,
            every, stat, stat, stat,
            pltpu.VMEM((GROUP * steps * heads, head_dim), jnp.float32),
            pltpu.VMEM((2, groups, heads // 2, 2 * rows, 2 * head_dim), jnp.bfloat16),
            pltpu.VMEM((tp_n, groups, tiles, rows, tile), jnp.bfloat16),
            pltpu.VMEM((groups, tiles // 2, rows, tile), jnp.bfloat16),
            dma((problems,)), dma((strips,)), dma((3,)), dma((groups,)), dma((8, chunks)), dma((8, chunks)),
            dma((max(tp_n - 1, 1), groups, tiles // 2)), dma((tp_n, groups, tiles)),
            dma((groups,)), dma((groups,)), dma((tp_n, groups, tiles // 2)),
        ],
        compiler_params=pltpu.CompilerParams(
            collective_id=0, has_side_effects=True, vmem_limit_bytes=67043328 - (2 << 20)
        ),
    )(lengths, winner, out_scales, flat, fresh, hidden_in, kv_cache, out_values)


def solution(mesh):
    placed = (
        P("cand", None, None),
        P("cand", None, "tp", None),
        P("cand", None, "tp", None, None),
        P("cand", "tp", None, None, None),
        P("cand"),
        P(),
        P("tp", None),
        P("tp", None),
    )
    return jax.shard_map(
        functools.partial(local, mesh.shape["cand"], mesh.shape["tp"]),
        mesh=mesh, in_specs=placed, out_specs=P("cand", None, None), check_vma=False,
    )
```
